32 devices in a mesh: ctx: 8 (over z, x), bit: 4 (over y, core).
Axes of the slice: x: 2, y: 2, z: 4, core: 2. Of those that a mesh axis runs over, the one named last changes fastest.
Arguments:
- query_proj: bfloat16 [4096, 4096], P(None, ('ctx', 'bit')), may hold values from -6 to 6
- key_proj: bfloat16 [4096, 4096], P(None, ('ctx', 'bit')), may hold values from -6 to 6
- value_proj: bfloat16 [4096, 4096], P(None, ('ctx', 'bit')), may hold values from -6 to 6
- filter_taps: bfloat16 [4096, 4096], P(None, ('ctx', 'bit')), may hold values from -0.09375 to 0.09375
- skip_gain: float32 [4096], replicated, may hold values from -4 to 4
Outputs:
- gated: bfloat16 [4096, 4096], P(None, ('ctx', 'bit'))
The draws below stay inside these ranges and needn't reach their ends.
All inputs are finite; a program needn't handle non-finite values.
Results may differ from the reference program's by a relative error of at most 0.0049.
Values may be sent and summed in bfloat16 or wider, within the bound.
No kernel may reach another device: no remote copies, remote signals or barrier semaphores. Data moves between devices by JAX's collectives and lax.ppermute only.
A program may use at most 128 MiB of HBM per device.

```python
import jax
import jax.numpy as jnp
from jax import lax

CH = 4096
SEQ = 4096
FFT_LEN = 8192


def level_of(own_key, extent, pieces, smallest, high):
    gain, own = 1.0, jax.random.fold_in(own_key, 6)
    for position, shards_of in pieces:
        draws = jnp.exp(jax.random.uniform(jax.random.fold_in(own, position), (shards_of,), jnp.float32, smallest / len(pieces), high / len(pieces)))
        gain = gain * jnp.repeat(draws, extent[position] // shards_of).reshape([-1 if axis == position else 1 for axis in range(len(extent))])
    return gain


def scatter_about(rng, shape, spread, reach, shards=(), kind=jnp.bfloat16):
    drawn = jax.random.normal(rng, shape, jnp.float32) * spread
    if len(shards) > 0:
        drawn = level_of(rng, shape, shards, -0.22, 0.18) * drawn
    return jnp.clip(drawn, min=-reach, max=reach).astype(kind)


def setup_inputs(seed: int = 0) -> dict:
    splits = jax.random.split(jax.random.key(seed), 6)
    return {
        "query_proj": scatter_about(splits[0], (CH, SEQ), 1.0, 6.0, ((1, 32),)),
        "key_proj": scatter_about(splits[1], (CH, SEQ), 1.0, 6.0, ((1, 32),)),
        "value_proj": scatter_about(splits[2], (CH, SEQ), 1.0, 6.0, ((1, 32),)),
        "filter_taps": scatter_about(splits[3], (CH, SEQ), SEQ ** -0.5, 0.09375, ((1, 32),)),
        "skip_gain": scatter_about(splits[4], (CH,), 1.0, 4.0, (), jnp.float32),
    }


def one_channel(pair_rows):
    prod_row, taps_row = pair_rows
    spectrum = jnp.fft.rfft(prod_row, n=FFT_LEN) * jnp.fft.rfft(taps_row, n=FFT_LEN)
    return jnp.fft.irfft(spectrum, n=FFT_LEN)[:SEQ]


def reference(query_proj, key_proj, value_proj, filter_taps, skip_gain):
    products = (key_proj.astype(jnp.float32) * value_proj.astype(jnp.float32)).astype(jnp.bfloat16)
    prod_float = products.astype(jnp.float32)
    convolution = lax.map(one_channel, (prod_float, filter_taps.astype(jnp.float32)))
    mixed = query_proj.astype(jnp.float32) * (convolution + skip_gain[:, None] * prod_float)
    return mixed.astype(jnp.bfloat16)
```

```python
import functools, math
import numpy as np
import jax, jax.numpy as jnp, ml_dtypes
from jax import lax
from jax.experimental import pallas as pl
from jax.sharding import PartitionSpec as P
from jax.experimental.pallas import tpu as pltpu

R2 = math.sqrt(0.5)
ROWS = [0, 8, 16, 24, 32] + [4, 20, 36, 52] + [1 + 8*m for m in range(8)] + [2 + 8*m for m in range(8)] + [3 + 8*m for m in range(8)]
NR = len(ROWS)

def split_np(t):
    hi = t.astype(ml_dtypes.bfloat16)
    lo = (t - hi.astype(np.float64)).astype(ml_dtypes.bfloat16)
    return hi, lo

@functools.lru_cache(None)
def tables():
    j = np.arange(128)
    th = 2*np.pi*((j[:, None]*j[None, :]) % 128)/128
    C, S = np.cos(th), np.sin(th)
    F = np.block([[C, -S], [S, C]])
    I = np.block([[C, S], [-S, C]])
    def trip(t):
        hi, lo = split_np(t)
        return np.concatenate([hi, hi, lo], 0)
    k = np.array(ROWS)
    ph = 2*np.pi*((k[:, None]*j[None, :]) % 8192)/8192
    w = np.where((k == 0) | (k == 32), 1.0, 2.0)[:, None]/8192
    twf = np.stack([np.cos(ph), -np.sin(ph)], 1).astype(np.float32)
    twi = np.stack([w*np.cos(ph), w*np.sin(ph)], 1).astype(np.float32)
    return trip(F), trip(I), twf, twi

def cadd(a, b): return (a[0]+b[0], a[1]+b[1])
def csub(a, b): return (a[0]-b[0], a[1]-b[1])
def cmulc(a, c, s):
    return (a[0]*c - a[1]*s, a[0]*s + a[1]*c)

def dft4(x, sg):
    a = cadd(x[0], x[2]); b = csub(x[0], x[2]); c = cadd(x[1], x[3]); d = csub(x[1], x[3])
    if sg < 0:
        return [cadd(a, c), (b[0]+d[1], b[1]-d[0]), csub(a, c), (b[0]-d[1], b[1]+d[0])]
    return [cadd(a, c), (b[0]-d[1], b[1]+d[0]), csub(a, c), (b[0]+d[1], b[1]-d[0])]

def dft8(x, sg):
    e = dft4([x[0], x[2], x[4], x[6]], sg); o = dft4([x[1], x[3], x[5], x[7]], sg)
    if sg < 0:
        o1 = ((o[1][0]+o[1][1])*R2, (o[1][1]-o[1][0])*R2)
        o2 = (o[2][1], -o[2][0])
        o3 = ((o[3][1]-o[3][0])*R2, -(o[3][0]+o[3][1])*R2)
        r2 = [(e[2][0]+o[2][1], e[2][1]-o[2][0]), (e[2][0]-o[2][1], e[2][1]+o[2][0])]
    else:
        o1 = ((o[1][0]-o[1][1])*R2, (o[1][0]+o[1][1])*R2)
        o3 = (-(o[3][0]+o[3][1])*R2, (o[3][0]-o[3][1])*R2)
        r2 = [(e[2][0]-o[2][1], e[2][1]+o[2][0]), (e[2][0]+o[2][1], e[2][1]-o[2][0])]
    return [cadd(e[0], o[0]), cadd(e[1], o1), r2[0], cadd(e[3], o3),
            csub(e[0], o[0]), csub(e[1], o1), r2[1], csub(e[3], o3)]

def tw64(n):
    a = 2*math.pi*n/64
    return math.cos(a), math.sin(a)

def fwd_stage1(a0, a1, a2, a3, n2):
    s = a0+a2; d = a0-a2; p = a1+a3; m = a1-a3
    mr = m*R2; pr = p*R2
    x0 = s+p; x4 = s-p
    x1 = (a0+mr, -a2-pr); x2 = (d, -m); x3 = (a0-mr, a2-pr)
    out = []
    for k1, x in ((1, x1), (2, x2), (3, x3)):
        if n2:
            c, sn = tw64(n2*k1); x = cmulc(x, c, -sn)
        out.append(x)
    return x0, x4, out

def fwd_rows_k0(v):
    a = v[0]+v[4]; b = v[0]-v[4]; c = v[2]+v[6]; d = v[2]-v[6]
    e = v[1]+v[5]; f = v[1]-v[5]; g = v[3]+v[7]; h = v[3]-v[7]
    z0 = (a+c)+(e+g); z4 = (a+c)-(e+g)
    z2 = (a-c, g-e)
    fh = (f-h)*R2; fg = (f+h)*R2
    z1 = (b+fh, -d-fg); z3 = (b-fh, d-fg)
    return [(z0, None), z1, z2, z3, (z4, None)]

def fwd_rows_k4(v):
    t = []
    for n in range(4):
        z = (v[n], -v[n+4])
        if n:
            c, s = math.cos(math.pi*n/8), math.sin(math.pi*n/8)
            z = cmulc(z, c, -s)
        t.append(z)
    return dft4(t, -1)

def inv_k0(z):
    z0, z1, z2, z3, z4 = z
    p = z0+z4; m = z0-z4
    a0 = p+z2[0]; a2 = p-z2[0]; a1 = m-z2[1]; a3 = m+z2[1]
    s = z1[0]+z3[0]; d = z1[0]-z3[0]; q = z1[1]+z3[1]; e = z1[1]-z3[1]
    b0 = s
    b1 = (d-q)*R2
    b2 = -e
    b3 = -(d+q)*R2
    return [a0+b0, a1+b1, a2+b2, a3+b3, a0-b0, a1-b1, a2-b2, a3-b3]

def inv_k4(g):
    s = dft4(g, 1)
    w = [None]*8
    for n in range(4):
        t = s[n]
        if n:
            c, sn = math.cos(math.pi*n/8), math.sin(math.pi*n/8)
            t = cmulc(t, c, sn)
        w[n] = t[0]; w[n+4] = -t[1]
    return w

def split(x):
    hi = x.astype(jnp.bfloat16)
    lo = (x - hi.astype(jnp.float32)).astype(jnp.bfloat16)
    return hi, lo

def conv_kernel(h_ref, x_ref, skip_ref, tf_ref, ti_ref, twf_ref, twi_ref, o_ref, ah, ax, ap, hf, xf, gf, G):
    f32 = jnp.float32
    def forward(src, a, dst):
        st0 = []; st4 = []; st = {1: [], 2: [], 3: []}
        for n2 in range(8):
            v = [src[8*n1+n2].astype(f32) for n1 in range(4)]
            x0, x4, xs = fwd_stage1(*v, n2)
            st0.append(x0); st4.append(x4)
            for k1 in (1, 2, 3): st[k1].append(xs[k1-1])
        def emit(i, z):
            c = twf_ref[i, 0:1, :]; s = twf_ref[i, 1:2, :]
            re, im = z
            if im is None:
                if ROWS[i] == 0:
                    r2, i2 = re, jnp.zeros_like(re)
                else:
                    r2, i2 = re*c, re*s
            else:
                r2, i2 = re*c - im*s, re*s + im*c
            for off, val in ((0, r2), (128, i2)):
                hi, lo = split(val)
                a[i*G:(i+1)*G, off:off+128] = hi
                a[i*G:(i+1)*G, 256+off:256+off+128] = lo
        for i, z in enumerate(fwd_rows_k0(st0)): emit(i, z)
        for i, z in enumerate(fwd_rows_k4(st4)): emit(5+i, z)
        for k1 in (1, 2, 3):
            for i, z in enumerate(dft8(st[k1], -1)): emit(9+8*(k1-1)+i, z)
    def mm(a, t_ref, dst):
        hi = a[:, 0:256]; lo = a[:, 256:512]
        dst[...] = jnp.dot(jnp.concatenate([hi, lo, hi], axis=1), t_ref[...], preferred_element_type=f32)
    forward(h_ref, ah, hf)
    mm(ah, tf_ref, hf)
    forward(x_ref, ax, xf)
    mm(ax, tf_ref, xf)
    for i in range(NR):
        sl = slice(i*G, (i+1)*G)
        hr = hf[sl, 0:128]; hi_ = hf[sl, 128:256]; xr = xf[sl, 0:128]; xi = xf[sl, 128:256]
        pr = hr*xr - hi_*xi; pi = hr*xi + hi_*xr
        for off, val in ((0, pr), (128, pi)):
            a, b = split(val)
            ap[sl, off:off+128] = a
            ap[sl, 256+off:256+off+128] = b
    mm(ap, ti_ref, gf)
    def get(i, real=False):
        sl = slice(i*G, (i+1)*G)
        re = gf[sl, 0:128]; im = gf[sl, 128:256]
        c = twi_ref[i, 0:1, :]; s = twi_ref[i, 1:2, :]
        if real:
            if ROWS[i] == 0: return re*c
            return re*c - im*s
        return (re*c - im*s, re*s + im*c)
    w0 = inv_k0([get(0, True), get(1), get(2), get(3), get(4, True)])
    w4 = inv_k4([get(5+i) for i in range(4)])
    V = {k1: dft8([get(9+8*(k1-1)+i) for i in range(8)], 1) for k1 in (1, 2, 3)}
    skip = skip_ref[...]
    for c2 in range(8):
        v1, v2, v3 = V[1][c2], V[2][c2], V[3][c2]
        if c2:
            v1, v2, v3 = [cmulc(v, *tw64(c2*k)) for k, v in ((1, v1), (2, v2), (3, v3))]
        p = w0[c2]+w4[c2]; m = w0[c2]-w4[c2]
        A = v1[0]+v3[0]; B = (v1[0]-v3[0])*R2; D = (v1[1]+v3[1])*R2; E = v1[1]-v3[1]
        ys = [p+v2[0]+A, m-v2[1]+(B-D), p-v2[0]-E, m+v2[1]-(B+D)]
        for c1 in range(4):
            n = 8*c1+c2
            o_ref[n] = (ys[c1] + skip*x_ref[n].astype(f32)).astype(o_ref.dtype)

def conv_call(r, skip, G=16, interpret=False):
    nb, ch2, L = r.shape
    ch = ch2//2
    tf, ti, twf, twi = [jnp.asarray(t) for t in tables()]
    ng = ch//G
    full = lambda a: pl.BlockSpec(a.shape, lambda g: (0,)*a.ndim)
    return pl.pallas_call(
        functools.partial(conv_kernel, G=G),
        out_shape=jax.ShapeDtypeStruct((nb, ch, L), jnp.bfloat16),
        grid=(ng,),
        in_specs=[pl.BlockSpec((nb, G, L), lambda g: (0, g, 0)),
                  pl.BlockSpec((nb, G, L), lambda g: (0, ng+g, 0)),
                  pl.BlockSpec((G, 1), lambda g: (g, 0)),
                  full(tf), full(ti), full(twf), full(twi)],
        out_specs=pl.BlockSpec((nb, G, L), lambda g: (0, g, 0)),
        scratch_shapes=[pltpu.VMEM((NR*G, 512), jnp.bfloat16)]*3 + [pltpu.VMEM((NR*G, 256), jnp.float32)]*3,
        compiler_params=pltpu.CompilerParams(vmem_limit_bytes=48 << 20),
        interpret=interpret,
        cost_estimate=pl.CostEstimate(flops=3*2*NR*ch*768*256, bytes_accessed=6*ch*L*nb, transcendentals=0),
    )(r, r, skip, tf, ti, twf, twi)

EXACT_MODE = lax.Precision.HIGHEST
FULL_TURN = 2.0 * math.pi


def rotation(left_index, right_index, length, orient):
    phases = left_index[:, None] * right_index[None, :] % length
    angles = orient * FULL_TURN / length * phases.astype(jnp.float32)
    return (jnp.cos(angles), jnp.sin(angles))


def contract(form, data, table):
    return jnp.einsum(form, data, table, precision=EXACT_MODE, preferred_element_type=jnp.float32)


def apply_table(form, real_part, imag_part, cos_table, sin_table):
    out_real = contract(form, real_part, cos_table) - contract(form, imag_part, sin_table)
    out_imag = contract(form, real_part, sin_table) + contract(form, imag_part, cos_table)
    return (out_real, out_imag)


def complex_times(a_real, a_imag, b_real, b_imag):
    return (a_real * b_real - a_imag * b_imag, a_real * b_imag + a_imag * b_real)


def conv_general(recv, skip):
    blocks, rows, length = recv.shape
    ch = rows // 2
    rows_fft = 2 * blocks
    total_len = rows_fft * length
    stacked = jnp.stack([recv[:, ch:], recv[:, :ch]]).astype(jnp.float32)
    positions = jnp.arange(length, dtype=jnp.int32)
    natural_rows = jnp.arange(rows_fft, dtype=jnp.int32)
    block_index = jnp.arange(blocks, dtype=jnp.int32)
    cos_fwd, sin_fwd = rotation(natural_rows, block_index, rows_fft, -1.0)
    spec_real = contract("gjcp,rj->grcp", stacked, cos_fwd)
    spec_imag = contract("gjcp,rj->grcp", stacked, sin_fwd)
    twist_cos, twist_sin = rotation(natural_rows, positions, total_len, -1.0)
    spec_real, spec_imag = complex_times(spec_real, spec_imag, twist_cos[None, :, None, :], twist_sin[None, :, None, :])
    low_cos, low_sin = rotation(positions, positions, length, -1.0)
    spec_real, spec_imag = apply_table("...p,pk->...k", spec_real, spec_imag, low_cos, low_sin)
    out_real, out_imag = complex_times(spec_real[0], spec_imag[0], spec_real[1], spec_imag[1])
    out_real, out_imag = apply_table("...k,pk->...p", out_real, out_imag, low_cos, -low_sin)
    out_real, out_imag = complex_times(out_real, out_imag, twist_cos[:, None, :], -twist_sin[:, None, :])
    inv_cos, inv_sin = rotation(block_index, natural_rows, rows_fft, 1.0)
    conv = (contract("rcp,jr->jcp", out_real, inv_cos) - contract("rcp,jr->jcp", out_imag, inv_sin)) / total_len
    return (conv + skip * stacked[0]).astype(jnp.bfloat16)


def on_device(query_proj, key_proj, value_proj, filter_taps, skip_gain):
    channels, length = query_proj.shape
    axes = ("ctx", "bit")
    devices_all = lax.axis_size("ctx") * lax.axis_size("bit")
    ch_dev = channels // devices_all
    products = (key_proj.astype(jnp.float32) * value_proj.astype(jnp.float32)).astype(jnp.bfloat16)
    send = jnp.concatenate(
        [filter_taps.reshape(devices_all, ch_dev, length), products.reshape(devices_all, ch_dev, length)], axis=1
    )
    recv = lax.all_to_all(send, axes, split_axis=0, concat_axis=0, tiled=True)
    mine = lax.axis_index(axes)
    skip = lax.dynamic_slice(skip_gain, (mine * ch_dev,), (ch_dev,))[:, None]
    if devices_all == 32 and length == 128 and ch_dev % 16 == 0:
        mixed = conv_call(recv, skip)
    else:
        mixed = conv_general(recv, skip)
    home = lax.all_to_all(mixed, axes, split_axis=0, concat_axis=0, tiled=True).reshape(channels, length)
    return (query_proj.astype(jnp.float32) * home.astype(jnp.float32)).astype(jnp.bfloat16)


def solution(mesh):
    placed = (P(None, ("ctx", "bit")),) * 4 + (P(),)
    return jax.shard_map(
        on_device, mesh=mesh, in_specs=placed, out_specs=P(None, ("ctx", "bit")), check_vma=False
    )
```

```python
import functools
import math

import jax
import jax.numpy as jnp
import ml_dtypes
import numpy as np
from jax import lax
from jax.experimental import pallas as pl
from jax.experimental.pallas import tpu as pltpu
from jax.sharding import PartitionSpec as P

BLOCKS, LANES, TOTAL = 32, 128, 8192
ROOT_HALF = math.sqrt(0.5)
COS8, SIN8 = math.cos(math.pi / 8), math.sin(math.pi / 8)


def split_table(table):
    high = table.astype(ml_dtypes.bfloat16)
    low = (table - high.astype(np.float64)).astype(ml_dtypes.bfloat16)
    return np.concatenate([high, high, low], axis=0)


@functools.lru_cache(None)
def tables():
    j = np.arange(LANES)
    angle = 2 * np.pi * (j[:, None] * j[None, :] % LANES) / LANES
    c, s = np.cos(angle), np.sin(angle)
    to_freq = split_table(np.block([[c, -s], [s, c]]))
    to_time = split_table(np.block([[c, s], [-s, c]]))
    m = (np.arange(4)[:, None] + 4 * np.arange(8)[None, :]).reshape(-1)
    twist = 2 * np.pi * ((4 * m + 1)[:, None] * j[None, :] % (2 * TOTAL)) / (2 * TOTAL)
    twist_in = np.stack([np.cos(twist), -np.sin(twist)], 1).astype(np.float32)
    twist_out = (2.0 / TOTAL * np.stack([np.cos(twist), np.sin(twist)], 1)).astype(np.float32)
    return to_freq, to_time, twist_in, twist_out


def cadd(a, b):
    return (a[0] + b[0], a[1] + b[1])


def csub(a, b):
    return (a[0] - b[0], a[1] - b[1])


def turn(a, numer, denom):
    if numer == 0:
        return a
    c, s = math.cos(math.pi * numer / denom), math.sin(math.pi * numer / denom)
    return (a[0] * c - a[1] * s, a[0] * s + a[1] * c)


def times_i(a, sign):
    return (-a[1], a[0]) if sign > 0 else (a[1], -a[0])


def dft4(x, sign):
    a, b, c, d = cadd(x[0], x[2]), csub(x[0], x[2]), cadd(x[1], x[3]), csub(x[1], x[3])
    if sign > 0:
        return [cadd(a, c), (b[0] - d[1], b[1] + d[0]), csub(a, c), (b[0] + d[1], b[1] - d[0])]
    return [cadd(a, c), (b[0] + d[1], b[1] - d[0]), csub(a, c), (b[0] - d[1], b[1] + d[0])]


def dft8(x, sign):
    e, o = dft4(x[0::2], sign), dft4(x[1::2], sign)
    p, q = o[1], o[3]
    if sign > 0:
        o1 = ((p[0] - p[1]) * ROOT_HALF, (p[0] + p[1]) * ROOT_HALF)
        o3 = ((q[0] + q[1]) * ROOT_HALF, (q[1] - q[0]) * ROOT_HALF)
        two = [(e[2][0] - o[2][1], e[2][1] + o[2][0]), (e[2][0] + o[2][1], e[2][1] - o[2][0])]
        three = [(e[3][0] - o3[0], e[3][1] - o3[1]), (e[3][0] + o3[0], e[3][1] + o3[1])]
    else:
        o1 = ((p[0] + p[1]) * ROOT_HALF, (p[1] - p[0]) * ROOT_HALF)
        o3 = ((q[0] - q[1]) * ROOT_HALF, (q[0] + q[1]) * ROOT_HALF)
        two = [(e[2][0] + o[2][1], e[2][1] - o[2][0]), (e[2][0] - o[2][1], e[2][1] + o[2][0])]
        three = [(e[3][0] - o3[0], e[3][1] - o3[1]), (e[3][0] + o3[0], e[3][1] + o3[1])]
    return [cadd(e[0], o[0]), cadd(e[1], o1), two[0], three[0], csub(e[0], o[0]), csub(e[1], o1), two[1], three[1]]


def first_stage(load, stage, group):
    for n2 in range(8):
        a0, a1, a2, a3 = [load(8 * n1 + n2) for n1 in range(4)]
        r = a2 * ROOT_HALF
        c1, s1, c3, s3 = a1 * COS8, a1 * SIN8, a3 * SIN8, a3 * COS8
        ar, br = a0 + r, a0 - r
        cr, ci, dr, di = c1 + c3, s1 + s3, c1 - c3, s3 - s1
        outs = [(ar + cr, -r - ci), (br + di, r - dr), (ar - cr, ci - r), (br - di, r + dr)]
        for m1 in range(4):
            put_row(stage, 8 * m1 + n2, group, turn(outs[m1], -n2 * (1 + 4 * m1), 64))


def put_row(dest, row, group, value):
    dest[row * group : (row + 1) * group, :LANES] = value[0]
    dest[row * group : (row + 1) * group, LANES:] = value[1]


def split(x):
    high = x.astype(jnp.bfloat16)
    return high, (x - high.astype(jnp.float32)).astype(jnp.bfloat16)


def put_split(dest, row, group, re, im):
    for at, part in ((0, re), (LANES, im)):
        high, low = split(part)
        dest[row * group : (row + 1) * group, at : at + LANES] = high
        dest[row * group : (row + 1) * group, 2 * LANES + at : 3 * LANES + at] = low


def twisted(values, m1, twist_ref):
    out = []
    for m2, (re, im) in enumerate(values):
        c, s = twist_ref[8 * m1 + m2, 0:1, :], twist_ref[8 * m1 + m2, 1:2, :]
        out.append((re * c - im * s, re * s + im * c))
    return out


def put_chunk(dest, m1, group, values):
    for m2, (re, im) in enumerate(values):
        put_split(dest, 8 * m1 + m2, group, re, im)


def apply_table(source, table_ref, dest, m1, group):
    rows = slice(8 * m1 * group, 8 * (m1 + 1) * group)
    high, low = source[rows, : 2 * LANES], source[rows, 2 * LANES :]
    dest[rows, :] = jnp.dot(
        jnp.concatenate([high, low, high], axis=1), table_ref[...], preferred_element_type=jnp.float32
    )


def get_chunk(source, m1, group):
    out = []
    for m2 in range(8):
        rows = slice((8 * m1 + m2) * group, (8 * m1 + m2 + 1) * group)
        out.append((source[rows, :LANES], source[rows, LANES:]))
    return out


def get_row(source, row, group):
    rows = slice(row * group, (row + 1) * group)
    return (source[rows, :LANES], source[rows, LANES:])


def last_stage(stage, skip, load, store, group):
    for n2 in range(8):
        v = [turn(get_row(stage, 8 * m1 + n2, group), n2 * (1 + 4 * m1), 64) for m1 in range(4)]
        a, b, c, d = cadd(v[0], v[2]), csub(v[0], v[2]), cadd(v[1], v[3]), csub(v[1], v[3])
        outs = [
            a[0] + c[0],
            (b[0] - d[1]) * COS8 - (b[1] + d[0]) * SIN8,
            ((a[0] - c[0]) - (a[1] - c[1])) * ROOT_HALF,
            (b[0] + d[1]) * SIN8 - (b[1] - d[0]) * COS8,
        ]
        for n1 in range(4):
            n = 8 * n1 + n2
            store(n, outs[n1] + skip * load(n))


def conv_kernel(r_ref, skip_ref, freq_ref, time_ref, tin_ref, tout_ref, o_ref, ta, pa, xa, tf, pf, xf, ts, ps, xs, group, ch):
    def body(g, carry):
        at = pl.multiple_of(g * group, group)
        mine = pl.ds(at, group)
        prods = pl.ds(pl.multiple_of(ch + at, group), group)

        def load_taps(n):
            return r_ref[n, mine, :].astype(jnp.float32)

        def load_prods(n):
            return r_ref[n, prods, :].astype(jnp.float32)

        def store(n, value):
            o_ref[n, mine, :] = value.astype(o_ref.dtype)

        first_stage(load_taps, ts, group)
        first_stage(load_prods, ps, group)

        def fwd(m1):
            put_chunk(ta, m1, group, twisted(dft8(get_chunk(ts, m1, group), -1), m1, tin_ref))
            apply_table(ta, freq_ref, tf, m1, group)
            put_chunk(pa, m1, group, twisted(dft8(get_chunk(ps, m1, group), -1), m1, tin_ref))
            apply_table(pa, freq_ref, pf, m1, group)

        def mid(m1):
            pairs = zip(get_chunk(tf, m1, group), get_chunk(pf, m1, group))
            put_chunk(xa, m1, group, [(a * c - b * d, a * d + b * c) for (a, b), (c, d) in pairs])
            apply_table(xa, time_ref, xf, m1, group)

        def bwd(m1):
            for m2, value in enumerate(dft8(twisted(get_chunk(xf, m1, group), m1, tout_ref), 1)):
                put_row(xs, 8 * m1 + m2, group, value)

        for step in range(6):
            if step < 4:
                fwd(step)
            if 0 <= step - 1 < 4:
                mid(step - 1)
            if 0 <= step - 2 < 4:
                bwd(step - 2)
        lane = lax.broadcasted_iota(jnp.int32, (group, ch), 1) - lax.broadcasted_iota(jnp.int32, (group, ch), 0)
        skip = jnp.sum(jnp.where(lane == at, skip_ref[...], 0.0), axis=1, keepdims=True)
        last_stage(xs, skip, load_prods, store, group)
        return carry

    lax.fori_loop(0, ch // group, body, 0)


def conv_call(recv, skip, group=16, interpret=False):
    blocks, rows, length = recv.shape
    ch = rows // 2
    whole = pl.BlockSpec(memory_space=pltpu.VMEM)
    return pl.pallas_call(
        functools.partial(conv_kernel, group=group, ch=ch),
        out_shape=jax.ShapeDtypeStruct((blocks, ch, length), jnp.bfloat16),
        in_specs=[whole] * 6,
        out_specs=whole,
        scratch_shapes=[pltpu.VMEM((BLOCKS * group, 4 * LANES), jnp.bfloat16)] * 3
        + [pltpu.VMEM((BLOCKS * group, 2 * LANES), jnp.float32)] * 6,
        compiler_params=pltpu.CompilerParams(vmem_limit_bytes=14 << 20),
        cost_estimate=pl.CostEstimate(
            flops=36 * BLOCKS * ch * 256 * 256, bytes_accessed=6 * BLOCKS * ch * LANES, transcendentals=0
        ),
        interpret=interpret,
    )(recv, skip, *[jnp.asarray(table) for table in tables()])


EXACT_MODE = lax.Precision.HIGHEST
FULL_TURN = 2.0 * math.pi


def rotation(left_index, right_index, length, orient):
    phases = left_index[:, None] * right_index[None, :] % length
    angles = orient * FULL_TURN / length * phases.astype(jnp.float32)
    return (jnp.cos(angles), jnp.sin(angles))


def contract(form, data, table):
    return jnp.einsum(form, data, table, precision=EXACT_MODE, preferred_element_type=jnp.float32)


def apply_rotation(form, real_part, imag_part, cos_table, sin_table):
    out_real = contract(form, real_part, cos_table) - contract(form, imag_part, sin_table)
    out_imag = contract(form, real_part, sin_table) + contract(form, imag_part, cos_table)
    return (out_real, out_imag)


def complex_times(a_real, a_imag, b_real, b_imag):
    return (a_real * b_real - a_imag * b_imag, a_real * b_imag + a_imag * b_real)


def conv_general(recv, skip):
    blocks, rows, length = recv.shape
    ch = rows // 2
    rows_fft = 2 * blocks
    total_len = rows_fft * length
    stacked = jnp.stack([recv[:, ch:], recv[:, :ch]]).astype(jnp.float32)
    positions = jnp.arange(length, dtype=jnp.int32)
    natural_rows = jnp.arange(rows_fft, dtype=jnp.int32)
    block_index = jnp.arange(blocks, dtype=jnp.int32)
    cos_fwd, sin_fwd = rotation(natural_rows, block_index, rows_fft, -1.0)
    spec_real = contract("gjcp,rj->grcp", stacked, cos_fwd)
    spec_imag = contract("gjcp,rj->grcp", stacked, sin_fwd)
    twist_cos, twist_sin = rotation(natural_rows, positions, total_len, -1.0)
    spec_real, spec_imag = complex_times(spec_real, spec_imag, twist_cos[None, :, None, :], twist_sin[None, :, None, :])
    low_cos, low_sin = rotation(positions, positions, length, -1.0)
    spec_real, spec_imag = apply_rotation("...p,pk->...k", spec_real, spec_imag, low_cos, low_sin)
    out_real, out_imag = complex_times(spec_real[0], spec_imag[0], spec_real[1], spec_imag[1])
    out_real, out_imag = apply_rotation("...k,pk->...p", out_real, out_imag, low_cos, -low_sin)
    out_real, out_imag = complex_times(out_real, out_imag, twist_cos[:, None, :], -twist_sin[:, None, :])
    inv_cos, inv_sin = rotation(block_index, natural_rows, rows_fft, 1.0)
    conv = (contract("rcp,jr->jcp", out_real, inv_cos) - contract("rcp,jr->jcp", out_imag, inv_sin)) / total_len
    return (conv + skip * stacked[0]).astype(jnp.bfloat16)


def on_device(query_proj, key_proj, value_proj, filter_taps, skip_gain):
    channels, length = query_proj.shape
    axes = ("ctx", "bit")
    devices_all = lax.axis_size("ctx") * lax.axis_size("bit")
    ch_dev = channels // devices_all
    products = key_proj * value_proj
    send = jnp.concatenate(
        [filter_taps.reshape(devices_all, ch_dev, length), products.reshape(devices_all, ch_dev, length)], axis=1
    )
    mine = lax.axis_index(axes)
    skip = lax.dynamic_slice(skip_gain, (mine * ch_dev,), (ch_dev,))[None, :]
    send, skip = lax.optimization_barrier((send, skip))
    recv = lax.all_to_all(send, axes, split_axis=0, concat_axis=0, tiled=True)
    if devices_all == 32 and length == 128 and ch_dev % 16 == 0:
        mixed = conv_call(recv, skip)
    else:
        mixed = conv_general(recv, skip.reshape(ch_dev, 1))
    home = lax.all_to_all(mixed, axes, split_axis=0, concat_axis=0, tiled=True).reshape(channels, length)
    return (query_proj.astype(jnp.float32) * home.astype(jnp.float32)).astype(jnp.bfloat16)


def solution(mesh):
    placed = (P(None, ("ctx", "bit")),) * 4 + (P(),)
    return jax.shard_map(
        on_device, mesh=mesh, in_specs=placed, out_specs=P(None, ("ctx", "bit")), check_vma=False
    )
```

```python
import functools
import itertools
import math

import jax
import jax.numpy as jnp
import ml_dtypes
import numpy as np
from jax import lax
from jax.experimental import pallas as pl
from jax.experimental.pallas import tpu as pltpu
from jax.sharding import PartitionSpec as P

BLOCKS, LANES, TOTAL = 32, 128, 8192
ROOT_HALF = math.sqrt(0.5)
COS8, SIN8 = math.cos(math.pi / 8), math.sin(math.pi / 8)


def split_table(table):
    high = table.astype(ml_dtypes.bfloat16)
    low = (table - high.astype(np.float64)).astype(ml_dtypes.bfloat16)
    return np.concatenate([high, high, low], axis=0)


@functools.lru_cache(None)
def tables():
    j = np.arange(LANES)
    angle = 2 * np.pi * (j[:, None] * j[None, :] % LANES) / LANES
    c, s = np.cos(angle), np.sin(angle)
    to_freq = split_table(np.block([[c, -s], [s, c]]))
    to_time = split_table(np.block([[c, s], [-s, c]]))
    m = (np.arange(4)[:, None] + 4 * np.arange(8)[None, :]).reshape(-1)
    twist = 2 * np.pi * ((4 * m + 1)[:, None] * j[None, :] % (2 * TOTAL)) / (2 * TOTAL)
    twist_in = np.stack([np.cos(twist), -np.sin(twist)], 1).astype(np.float32)
    twist_out = (2.0 / TOTAL * np.stack([np.cos(twist), np.sin(twist)], 1)).astype(np.float32)
    return to_freq, to_time, twist_in, twist_out


def cadd(a, b):
    return (a[0] + b[0], a[1] + b[1])


def csub(a, b):
    return (a[0] - b[0], a[1] - b[1])


def turn(a, numer, denom):
    if numer == 0:
        return a
    c, s = math.cos(math.pi * numer / denom), math.sin(math.pi * numer / denom)
    return (a[0] * c - a[1] * s, a[0] * s + a[1] * c)


def times_i(a, sign):
    return (-a[1], a[0]) if sign > 0 else (a[1], -a[0])


def dft4(x, sign):
    a, b, c, d = cadd(x[0], x[2]), csub(x[0], x[2]), cadd(x[1], x[3]), csub(x[1], x[3])
    if sign > 0:
        return [cadd(a, c), (b[0] - d[1], b[1] + d[0]), csub(a, c), (b[0] + d[1], b[1] - d[0])]
    return [cadd(a, c), (b[0] + d[1], b[1] - d[0]), csub(a, c), (b[0] - d[1], b[1] + d[0])]


def dft8(x, sign):
    e, o = dft4(x[0::2], sign), dft4(x[1::2], sign)
    p, q = o[1], o[3]
    if sign > 0:
        o1 = ((p[0] - p[1]) * ROOT_HALF, (p[0] + p[1]) * ROOT_HALF)
        o3 = ((q[0] + q[1]) * ROOT_HALF, (q[1] - q[0]) * ROOT_HALF)
        two = [(e[2][0] - o[2][1], e[2][1] + o[2][0]), (e[2][0] + o[2][1], e[2][1] - o[2][0])]
        three = [(e[3][0] - o3[0], e[3][1] - o3[1]), (e[3][0] + o3[0], e[3][1] + o3[1])]
    else:
        o1 = ((p[0] + p[1]) * ROOT_HALF, (p[1] - p[0]) * ROOT_HALF)
        o3 = ((q[0] - q[1]) * ROOT_HALF, (q[0] + q[1]) * ROOT_HALF)
        two = [(e[2][0] + o[2][1], e[2][1] - o[2][0]), (e[2][0] - o[2][1], e[2][1] + o[2][0])]
        three = [(e[3][0] - o3[0], e[3][1] - o3[1]), (e[3][0] + o3[0], e[3][1] + o3[1])]
    return [cadd(e[0], o[0]), cadd(e[1], o1), two[0], three[0], csub(e[0], o[0]), csub(e[1], o1), two[1], three[1]]


def first_stage(load, stage, group):
    for n2 in range(8):
        a0, a1, a2, a3 = [load(8 * n1 + n2) for n1 in range(4)]
        r = a2 * ROOT_HALF
        c1, s1, c3, s3 = a1 * COS8, a1 * SIN8, a3 * SIN8, a3 * COS8
        ar, br = a0 + r, a0 - r
        cr, ci, dr, di = c1 + c3, s1 + s3, c1 - c3, s3 - s1
        outs = [(ar + cr, -r - ci), (br + di, r - dr), (ar - cr, ci - r), (br - di, r + dr)]
        for m1 in range(4):
            put_row(stage, 8 * m1 + n2, group, turn(outs[m1], -n2 * (1 + 4 * m1), 64))


def put_row(dest, row, group, value):
    dest[row * group : (row + 1) * group, :LANES] = value[0]
    dest[row * group : (row + 1) * group, LANES:] = value[1]


def split(x):
    high = x.astype(jnp.bfloat16)
    return high, (x - high.astype(jnp.float32)).astype(jnp.bfloat16)


def put_split(dest, row, group, re, im):
    for at, part in ((0, re), (LANES, im)):
        high, low = split(part)
        dest[row * group : (row + 1) * group, at : at + LANES] = high
        dest[row * group : (row + 1) * group, 2 * LANES + at : 3 * LANES + at] = low


def twisted(values, m1, twist_ref):
    out = []
    for m2, (re, im) in enumerate(values):
        c, s = twist_ref[8 * m1 + m2, 0:1, :], twist_ref[8 * m1 + m2, 1:2, :]
        out.append((re * c - im * s, re * s + im * c))
    return out


def put_chunk(dest, m1, group, values):
    for m2, (re, im) in enumerate(values):
        put_split(dest, 8 * m1 + m2, group, re, im)


def apply_table(source, table_ref, dest, m1, group):
    rows = slice(8 * m1 * group, 8 * (m1 + 1) * group)
    high, low = source[rows, : 2 * LANES], source[rows, 2 * LANES :]
    dest[rows, :] = jnp.dot(
        jnp.concatenate([high, low, high], axis=1), table_ref[...], preferred_element_type=jnp.float32
    )


def get_chunk(source, m1, group):
    out = []
    for m2 in range(8):
        rows = slice((8 * m1 + m2) * group, (8 * m1 + m2 + 1) * group)
        out.append((source[rows, :LANES], source[rows, LANES:]))
    return out


def get_row(source, row, group):
    rows = slice(row * group, (row + 1) * group)
    return (source[rows, :LANES], source[rows, LANES:])


def last_stage(stage, skip, load, store, group):
    for n2 in range(8):
        v = [turn(get_row(stage, 8 * m1 + n2, group), n2 * (1 + 4 * m1), 64) for m1 in range(4)]
        a, b, c, d = cadd(v[0], v[2]), csub(v[0], v[2]), cadd(v[1], v[3]), csub(v[1], v[3])
        outs = [
            a[0] + c[0],
            (b[0] - d[1]) * COS8 - (b[1] + d[0]) * SIN8,
            ((a[0] - c[0]) - (a[1] - c[1])) * ROOT_HALF,
            (b[0] + d[1]) * SIN8 - (b[1] - d[0]) * COS8,
        ]
        for n1 in range(4):
            n = 8 * n1 + n2
            store(n, outs[n1] + skip * load(n))


def conv_kernel(r_ref, skip_ref, freq_ref, time_ref, tin_ref, tout_ref, o_ref, *scratch, group, ch):
    ta, pa, xa, xf, ts, ps, xs = scratch[:7]
    tf, pf = scratch[7:9], scratch[9:11]
    steps = ch // group

    def rows(g, base=0):
        return slice(base + g * group, base + (g + 1) * group)

    def loader(g, base):
        return lambda n: r_ref[n, rows(g, base), :].astype(jnp.float32)

    def storer(g):
        def store(n, value):
            o_ref[n, rows(g), :] = value.astype(o_ref.dtype)

        return store

    def head(g):
        def fwd(stage, a, f, m1):
            put_chunk(a, m1, group, twisted(dft8(get_chunk(stage, m1, group), -1), m1, tin_ref))
            apply_table(a, freq_ref, f, m1, group)

        yield lambda: first_stage(loader(g, 0), ts, group)
        yield lambda: first_stage(loader(g, ch), ps, group)
        for m1 in range(4):
            yield lambda: fwd(ts, ta, tf[g % 2], m1)
            yield lambda: fwd(ps, pa, pf[g % 2], m1)

    def tail(g):
        def mid(m1):
            pairs = zip(get_chunk(tf[g % 2], m1, group), get_chunk(pf[g % 2], m1, group))
            put_chunk(xa, m1, group, [(a * c - b * d, a * d + b * c) for (a, b), (c, d) in pairs])
            apply_table(xa, time_ref, xf, m1, group)

        def bwd(m1):
            for m2, value in enumerate(dft8(twisted(get_chunk(xf, m1, group), m1, tout_ref), 1)):
                put_row(xs, 8 * m1 + m2, group, value)

        def last():
            lane = lax.broadcasted_iota(jnp.int32, (group, ch), 1) - lax.broadcasted_iota(jnp.int32, (group, ch), 0)
            skip = jnp.sum(jnp.where(lane == g * group, skip_ref[...], 0.0), axis=1, keepdims=True)
            last_stage(xs, skip, loader(g, ch), storer(g), group)

        yield lambda: mid(0)
        yield lambda: mid(1)
        yield lambda: mid(2)
        yield lambda: bwd(0)
        yield lambda: mid(3)
        yield lambda: bwd(1)
        yield lambda: bwd(2)
        yield lambda: bwd(3)
        yield last

    for g in range(steps + 1):
        streams = [tail(g - 1)] if g > 0 else []
        streams += [head(g)] if g < steps else []
        for now in itertools.zip_longest(*streams):
            for piece in now:
                if piece is not None:
                    piece()


def conv_call(recv, skip, group=16, interpret=False):
    blocks, rows, length = recv.shape
    ch = rows // 2
    whole = pl.BlockSpec(memory_space=pltpu.VMEM)
    return pl.pallas_call(
        functools.partial(conv_kernel, group=group, ch=ch),
        out_shape=jax.ShapeDtypeStruct((blocks, ch, length), jnp.bfloat16),
        in_specs=[whole] * 6,
        out_specs=whole,
        scratch_shapes=[pltpu.VMEM((BLOCKS * group, 4 * LANES), jnp.bfloat16)] * 3
        + [pltpu.VMEM((BLOCKS * group, 2 * LANES), jnp.float32)] * 8,
        compiler_params=pltpu.CompilerParams(vmem_limit_bytes=14 << 20),
        cost_estimate=pl.CostEstimate(
            flops=36 * BLOCKS * ch * 256 * 256, bytes_accessed=6 * BLOCKS * ch * LANES, transcendentals=0
        ),
        interpret=interpret,
    )(recv, skip, *[jnp.asarray(table) for table in tables()])


EXACT_MODE = lax.Precision.HIGHEST
FULL_TURN = 2.0 * math.pi


def rotation(left_index, right_index, length, orient):
    phases = left_index[:, None] * right_index[None, :] % length
    angles = orient * FULL_TURN / length * phases.astype(jnp.float32)
    return (jnp.cos(angles), jnp.sin(angles))


def contract(form, data, table):
    return jnp.einsum(form, data, table, precision=EXACT_MODE, preferred_element_type=jnp.float32)


def apply_rotation(form, real_part, imag_part, cos_table, sin_table):
    out_real = contract(form, real_part, cos_table) - contract(form, imag_part, sin_table)
    out_imag = contract(form, real_part, sin_table) + contract(form, imag_part, cos_table)
    return (out_real, out_imag)


def complex_times(a_real, a_imag, b_real, b_imag):
    return (a_real * b_real - a_imag * b_imag, a_real * b_imag + a_imag * b_real)


def conv_general(recv, skip):
    blocks, rows, length = recv.shape
    ch = rows // 2
    rows_fft = 2 * blocks
    total_len = rows_fft * length
    stacked = jnp.stack([recv[:, ch:], recv[:, :ch]]).astype(jnp.float32)
    positions = jnp.arange(length, dtype=jnp.int32)
    natural_rows = jnp.arange(rows_fft, dtype=jnp.int32)
    block_index = jnp.arange(blocks, dtype=jnp.int32)
    cos_fwd, sin_fwd = rotation(natural_rows, block_index, rows_fft, -1.0)
    spec_real = contract("gjcp,rj->grcp", stacked, cos_fwd)
    spec_imag = contract("gjcp,rj->grcp", stacked, sin_fwd)
    twist_cos, twist_sin = rotation(natural_rows, positions, total_len, -1.0)
    spec_real, spec_imag = complex_times(spec_real, spec_imag, twist_cos[None, :, None, :], twist_sin[None, :, None, :])
    low_cos, low_sin = rotation(positions, positions, length, -1.0)
    spec_real, spec_imag = apply_rotation("...p,pk->...k", spec_real, spec_imag, low_cos, low_sin)
    out_real, out_imag = complex_times(spec_real[0], spec_imag[0], spec_real[1], spec_imag[1])
    out_real, out_imag = apply_rotation("...k,pk->...p", out_real, out_imag, low_cos, -low_sin)
    out_real, out_imag = complex_times(out_real, out_imag, twist_cos[:, None, :], -twist_sin[:, None, :])
    inv_cos, inv_sin = rotation(block_index, natural_rows, rows_fft, 1.0)
    conv = (contract("rcp,jr->jcp", out_real, inv_cos) - contract("rcp,jr->jcp", out_imag, inv_sin)) / total_len
    return (conv + skip * stacked[0]).astype(jnp.bfloat16)


def on_device(query_proj, key_proj, value_proj, filter_taps, skip_gain):
    channels, length = query_proj.shape
    axes = ("ctx", "bit")
    devices_all = lax.axis_size("ctx") * lax.axis_size("bit")
    ch_dev = channels // devices_all
    products = key_proj * value_proj
    send = jnp.concatenate(
        [filter_taps.reshape(devices_all, ch_dev, length), products.reshape(devices_all, ch_dev, length)], axis=1
    )
    mine = lax.axis_index(axes)
    skip = lax.dynamic_slice(skip_gain, (mine * ch_dev,), (ch_dev,))[None, :]
    send, skip = lax.optimization_barrier((send, skip))
    recv = lax.all_to_all(send, axes, split_axis=0, concat_axis=0, tiled=True)
    if devices_all == 32 and length == 128 and ch_dev % 16 == 0:
        mixed = conv_call(recv, skip)
    else:
        mixed = conv_general(recv, skip.reshape(ch_dev, 1))
    home = lax.all_to_all(mixed, axes, split_axis=0, concat_axis=0, tiled=True).reshape(channels, length)
    return (query_proj.astype(jnp.float32) * home.astype(jnp.float32)).astype(jnp.bfloat16)


def solution(mesh):
    placed = (P(None, ("ctx", "bit")),) * 4 + (P(),)
    return jax.shard_map(
        on_device, mesh=mesh, in_specs=placed, out_specs=P(None, ("ctx", "bit")), check_vma=False
    )
```

```python
import functools
import itertools
import math

import jax
import jax.numpy as jnp
import ml_dtypes
import numpy as np
from jax import lax
from jax.experimental import pallas as pl
from jax.experimental.pallas import tpu as pltpu
from jax.sharding import PartitionSpec as P

BLOCKS, LANES, TOTAL = 32, 128, 8192
ROOT_HALF = math.sqrt(0.5)
COS8, SIN8 = math.cos(math.pi / 8), math.sin(math.pi / 8)


def split_table(table):
    high = table.astype(ml_dtypes.bfloat16)
    low = (table - high.astype(np.float64)).astype(ml_dtypes.bfloat16)
    return np.concatenate([high, high, low], axis=0)


@functools.lru_cache(None)
def tables():
    j = np.arange(LANES)
    angle = 2 * np.pi * (j[:, None] * j[None, :] % LANES) / LANES
    c, s = np.cos(angle), np.sin(angle)
    to_freq = split_table(np.block([[c, -s], [s, c]]))
    to_time = split_table(np.block([[c, s], [-s, c]]))
    m = (np.arange(4)[:, None] + 4 * np.arange(8)[None, :]).reshape(-1)
    twist = 2 * np.pi * ((4 * m + 1)[:, None] * j[None, :] % (2 * TOTAL)) / (2 * TOTAL)
    twist_in = np.stack([np.cos(twist), -np.sin(twist)], 1).astype(np.float32)
    twist_out = (2.0 / TOTAL * np.stack([np.cos(twist), np.sin(twist)], 1)).astype(np.float32)
    return to_freq, to_time, twist_in, twist_out


def cadd(a, b):
    return (a[0] + b[0], a[1] + b[1])


def csub(a, b):
    return (a[0] - b[0], a[1] - b[1])


def turn(a, numer, denom):
    if numer == 0:
        return a
    c, s = math.cos(math.pi * numer / denom), math.sin(math.pi * numer / denom)
    return (a[0] * c - a[1] * s, a[0] * s + a[1] * c)


def times_i(a, sign):
    return (-a[1], a[0]) if sign > 0 else (a[1], -a[0])


def dft4(x, sign):
    a, b, c, d = cadd(x[0], x[2]), csub(x[0], x[2]), cadd(x[1], x[3]), csub(x[1], x[3])
    if sign > 0:
        return [cadd(a, c), (b[0] - d[1], b[1] + d[0]), csub(a, c), (b[0] + d[1], b[1] - d[0])]
    return [cadd(a, c), (b[0] + d[1], b[1] - d[0]), csub(a, c), (b[0] - d[1], b[1] + d[0])]


def dft8(x, sign):
    e, o = dft4(x[0::2], sign), dft4(x[1::2], sign)
    p, q = o[1], o[3]
    if sign > 0:
        o1 = ((p[0] - p[1]) * ROOT_HALF, (p[0] + p[1]) * ROOT_HALF)
        o3 = ((q[0] + q[1]) * ROOT_HALF, (q[1] - q[0]) * ROOT_HALF)
        two = [(e[2][0] - o[2][1], e[2][1] + o[2][0]), (e[2][0] + o[2][1], e[2][1] - o[2][0])]
        three = [(e[3][0] - o3[0], e[3][1] - o3[1]), (e[3][0] + o3[0], e[3][1] + o3[1])]
    else:
        o1 = ((p[0] + p[1]) * ROOT_HALF, (p[1] - p[0]) * ROOT_HALF)
        o3 = ((q[0] - q[1]) * ROOT_HALF, (q[0] + q[1]) * ROOT_HALF)
        two = [(e[2][0] + o[2][1], e[2][1] - o[2][0]), (e[2][0] - o[2][1], e[2][1] + o[2][0])]
        three = [(e[3][0] - o3[0], e[3][1] - o3[1]), (e[3][0] + o3[0], e[3][1] + o3[1])]
    return [cadd(e[0], o[0]), cadd(e[1], o1), two[0], three[0], csub(e[0], o[0]), csub(e[1], o1), two[1], three[1]]


def first_stage(load, stage, group):
    for n2 in range(8):
        a0, a1, a2, a3 = [load(8 * n1 + n2) for n1 in range(4)]
        r = a2 * ROOT_HALF
        c1, s1, c3, s3 = a1 * COS8, a1 * SIN8, a3 * SIN8, a3 * COS8
        ar, br = a0 + r, a0 - r
        cr, ci, dr, di = c1 + c3, s1 + s3, c1 - c3, s3 - s1
        outs = [(ar + cr, -r - ci), (br + di, r - dr), (ar - cr, ci - r), (br - di, r + dr)]
        for m1 in range(4):
            put_row(stage, 8 * m1 + n2, group, turn(outs[m1], -n2 * (1 + 4 * m1), 64))


def put_row(dest, row, group, value):
    dest[row * group : (row + 1) * group, :LANES] = value[0]
    dest[row * group : (row + 1) * group, LANES:] = value[1]


def split(x):
    high = x.astype(jnp.bfloat16)
    return high, (x - high.astype(jnp.float32)).astype(jnp.bfloat16)


def put_split(dest, row, group, re, im):
    for at, part in ((0, re), (LANES, im)):
        high, low = split(part)
        dest[row * group : (row + 1) * group, at : at + LANES] = high
        dest[row * group : (row + 1) * group, 2 * LANES + at : 3 * LANES + at] = low


def twisted(values, m1, twist_ref):
    out = []
    for m2, (re, im) in enumerate(values):
        c, s = twist_ref[8 * m1 + m2, 0:1, :], twist_ref[8 * m1 + m2, 1:2, :]
        out.append((re * c - im * s, re * s + im * c))
    return out


def put_chunk(dest, m1, group, values):
    for m2, (re, im) in enumerate(values):
        put_split(dest, 8 * m1 + m2, group, re, im)


def apply_table(source, table_ref, dest, m1, group):
    rows = slice(8 * m1 * group, 8 * (m1 + 1) * group)
    high, low = source[rows, : 2 * LANES], source[rows, 2 * LANES :]
    dest[rows, :] = jnp.dot(
        jnp.concatenate([high, low, high], axis=1), table_ref[...], preferred_element_type=jnp.float32
    )


def get_chunk(source, m1, group):
    out = []
    for m2 in range(8):
        rows = slice((8 * m1 + m2) * group, (8 * m1 + m2 + 1) * group)
        out.append((source[rows, :LANES], source[rows, LANES:]))
    return out


def get_row(source, row, group):
    rows = slice(row * group, (row + 1) * group)
    return (source[rows, :LANES], source[rows, LANES:])


def last_stage(stage, skip, load, store, group):
    for n2 in range(8):
        v = [turn(get_row(stage, 8 * m1 + n2, group), n2 * (1 + 4 * m1), 64) for m1 in range(4)]
        a, b, c, d = cadd(v[0], v[2]), csub(v[0], v[2]), cadd(v[1], v[3]), csub(v[1], v[3])
        outs = [
            a[0] + c[0],
            (b[0] - d[1]) * COS8 - (b[1] + d[0]) * SIN8,
            ((a[0] - c[0]) - (a[1] - c[1])) * ROOT_HALF,
            (b[0] + d[1]) * SIN8 - (b[1] - d[0]) * COS8,
        ]
        for n1 in range(4):
            n = 8 * n1 + n2
            store(n, outs[n1] + skip * load(n))


def conv_kernel(r_ref, skip_ref, freq_ref, time_ref, tin_ref, tout_ref, o_ref, *scratch, group, ch):
    ta, pa, xa, xf, ts, ps, xs = scratch[:7]
    tf, pf = scratch[7:9], scratch[9:11]
    steps = ch // group

    def rows(g, base=0):
        return slice(base + g * group, base + (g + 1) * group)

    def loader(g, base):
        return lambda n: r_ref[n, rows(g, base), :].astype(jnp.float32)

    def storer(g):
        def store(n, value):
            o_ref[n, rows(g), :] = value.astype(o_ref.dtype)

        return store

    def head(g):
        def fwd(stage, a, f, m1):
            put_chunk(a, m1, group, twisted(dft8(get_chunk(stage, m1, group), -1), m1, tin_ref))
            apply_table(a, freq_ref, f, m1, group)

        yield lambda: first_stage(loader(g, 0), ts, group)
        yield lambda: first_stage(loader(g, ch), ps, group)
        for m1 in range(4):
            yield lambda: fwd(ts, ta, tf[g % 2], m1)
            yield lambda: fwd(ps, pa, pf[g % 2], m1)

    def tail(g):
        def mid(m1):
            pairs = zip(get_chunk(tf[g % 2], m1, group), get_chunk(pf[g % 2], m1, group))
            put_chunk(xa, m1, group, [(a * c - b * d, a * d + b * c) for (a, b), (c, d) in pairs])
            apply_table(xa, time_ref, xf, m1, group)

        def bwd(m1):
            for m2, value in enumerate(dft8(twisted(get_chunk(xf, m1, group), m1, tout_ref), 1)):
                put_row(xs, 8 * m1 + m2, group, value)

        def last():
            lane = lax.broadcasted_iota(jnp.int32, (group, ch), 1) - lax.broadcasted_iota(jnp.int32, (group, ch), 0)
            skip = jnp.sum(jnp.where(lane == g * group, skip_ref[...], 0.0), axis=1, keepdims=True)
            last_stage(xs, skip, loader(g, ch), storer(g), group)

        yield lambda: mid(0)
        yield lambda: mid(1)
        yield lambda: mid(2)
        yield lambda: bwd(0)
        yield lambda: mid(3)
        yield lambda: bwd(1)
        yield lambda: bwd(2)
        yield lambda: bwd(3)
        yield last

    for g in range(steps + 1):
        streams = [tail(g - 1)] if g > 0 else []
        streams += [head(g)] if g < steps else []
        for now in itertools.zip_longest(*streams):
            for piece in now:
                if piece is not None:
                    piece()


def conv_call(recv, skip, group=16, interpret=False):
    blocks, rows, length = recv.shape
    ch = rows // 2
    whole = pl.BlockSpec(memory_space=pltpu.VMEM)
    return pl.pallas_call(
        functools.partial(conv_kernel, group=group, ch=ch),
        out_shape=jax.ShapeDtypeStruct((blocks, ch, length), jnp.bfloat16),
        in_specs=[whole] * 6,
        out_specs=whole,
        scratch_shapes=[pltpu.VMEM((BLOCKS * group, 4 * LANES), jnp.bfloat16)] * 3
        + [pltpu.VMEM((BLOCKS * group, 2 * LANES), jnp.float32)] * 8,
        compiler_params=pltpu.CompilerParams(vmem_limit_bytes=14 << 20),
        cost_estimate=pl.CostEstimate(
            flops=36 * BLOCKS * ch * 256 * 256, bytes_accessed=6 * BLOCKS * ch * LANES, transcendentals=0
        ),
        interpret=interpret,
    )(recv, skip, *[jnp.asarray(table) for table in tables()])


EXACT_MODE = lax.Precision.HIGHEST
FULL_TURN = 2.0 * math.pi


def rotation(left_index, right_index, length, orient):
    phases = left_index[:, None] * right_index[None, :] % length
    angles = orient * FULL_TURN / length * phases.astype(jnp.float32)
    return (jnp.cos(angles), jnp.sin(angles))


def contract(form, data, table):
    return jnp.einsum(form, data, table, precision=EXACT_MODE, preferred_element_type=jnp.float32)


def apply_rotation(form, real_part, imag_part, cos_table, sin_table):
    out_real = contract(form, real_part, cos_table) - contract(form, imag_part, sin_table)
    out_imag = contract(form, real_part, sin_table) + contract(form, imag_part, cos_table)
    return (out_real, out_imag)


def complex_times(a_real, a_imag, b_real, b_imag):
    return (a_real * b_real - a_imag * b_imag, a_real * b_imag + a_imag * b_real)


def conv_general(recv, skip):
    blocks, rows, length = recv.shape
    ch = rows // 2
    rows_fft = 2 * blocks
    total_len = rows_fft * length
    stacked = jnp.stack([recv[:, ch:], recv[:, :ch]]).astype(jnp.float32)
    positions = jnp.arange(length, dtype=jnp.int32)
    natural_rows = jnp.arange(rows_fft, dtype=jnp.int32)
    block_index = jnp.arange(blocks, dtype=jnp.int32)
    cos_fwd, sin_fwd = rotation(natural_rows, block_index, rows_fft, -1.0)
    spec_real = contract("gjcp,rj->grcp", stacked, cos_fwd)
    spec_imag = contract("gjcp,rj->grcp", stacked, sin_fwd)
    twist_cos, twist_sin = rotation(natural_rows, positions, total_len, -1.0)
    spec_real, spec_imag = complex_times(spec_real, spec_imag, twist_cos[None, :, None, :], twist_sin[None, :, None, :])
    low_cos, low_sin = rotation(positions, positions, length, -1.0)
    spec_real, spec_imag = apply_rotation("...p,pk->...k", spec_real, spec_imag, low_cos, low_sin)
    out_real, out_imag = complex_times(spec_real[0], spec_imag[0], spec_real[1], spec_imag[1])
    out_real, out_imag = apply_rotation("...k,pk->...p", out_real, out_imag, low_cos, -low_sin)
    out_real, out_imag = complex_times(out_real, out_imag, twist_cos[:, None, :], -twist_sin[:, None, :])
    inv_cos, inv_sin = rotation(block_index, natural_rows, rows_fft, 1.0)
    conv = (contract("rcp,jr->jcp", out_real, inv_cos) - contract("rcp,jr->jcp", out_imag, inv_sin)) / total_len
    return (conv + skip * stacked[0]).astype(jnp.bfloat16)


def on_device(query_proj, key_proj, value_proj, filter_taps, skip_gain):
    channels, length = query_proj.shape
    axes = ("ctx", "bit")
    devices_all = lax.axis_size("ctx") * lax.axis_size("bit")
    ch_dev = channels // devices_all
    products, gain = lax.optimization_barrier((key_proj * value_proj, skip_gain))
    send = jnp.concatenate(
        [filter_taps.reshape(devices_all, ch_dev, length), products.reshape(devices_all, ch_dev, length)], axis=1
    )
    mine = lax.axis_index(axes)
    skip = lax.dynamic_slice(gain, (mine * ch_dev,), (ch_dev,))[None, :]
    send, skip = lax.optimization_barrier((send, skip))
    recv = lax.all_to_all(send, axes, split_axis=0, concat_axis=0, tiled=True)
    if devices_all == 32 and length == 128 and ch_dev % 16 == 0:
        mixed = conv_call(recv, skip)
    else:
        mixed = conv_general(recv, skip.reshape(ch_dev, 1))
    home = lax.all_to_all(mixed, axes, split_axis=0, concat_axis=0, tiled=True).reshape(channels, length)
    return (query_proj.astype(jnp.float32) * home.astype(jnp.float32)).astype(jnp.bfloat16)


def solution(mesh):
    placed = (P(None, ("ctx", "bit")),) * 4 + (P(),)
    return jax.shard_map(
        on_device, mesh=mesh, in_specs=placed, out_specs=P(None, ("ctx", "bit")), check_vma=False
    )
```
